32 devices in a mesh: grp: 8 (over z, y), mem: 4 (over x, core).
Axes of the slice: x: 2, y: 2, z: 4, core: 2. Of those that a mesh axis runs over, the one named last changes fastest.
Arguments:
- codes: bfloat16 [8192, 1024], P(('grp', 'mem')), as said below
- scales: float32 [8192, 8], P(('grp', 'mem')), may hold values from 0.2 to 2
- cluster_id: int32 [8192], P(('grp', 'mem')), may hold values from 0 to 63, as said below
Outputs:
- smoothed: bfloat16 [8192, 1024], P(('grp', 'mem'))
- dup_mass: bfloat16 [8192], P(('grp', 'mem'))
The draws below stay inside these ranges and needn't reach their ends.
Inputs may be any that keep to these rules, and one draw needn't show every extreme that they name: `cluster_id`: cluster c belongs to owner group c mod 8. Among the 256 documents of one device, at most 40 belong to clusters of any one owner group, and at most 20 to any one cluster; for each index along mem, some owner group gets exactly 40 from every device of that index, and some cluster of that group exactly 20 from every device of that index. `codes`: documents of one cluster lie near a common direction.
All inputs are finite; a program needn't handle non-finite values.
Results may differ from the reference program's by a relative error of at most 0.0034.
Values may be sent and summed in bfloat16 or wider, within the bound.
No kernel may reach another device: no remote copies, remote signals or barrier semaphores. Data moves between devices by JAX's collectives and lax.ppermute only.
A program may use at most 64 MiB of HBM per device.

```python
import math
import jax
import jax.numpy as jnp
from jax import lax

D = 1024
BLOCK = 128
CL_GRP = 8
ROWS = 256
CAP = 40
KCAP = 20
CLUSTERS = 64
NROWS = 8192
N_GRP = 8
N_MEM = 4


def assign_clusters(key):
    devices = N_GRP * N_MEM
    hot_perm = jax.random.permutation(jax.random.fold_in(key, 11), N_GRP)
    device = jnp.arange(devices, dtype=jnp.int32)
    hot = hot_perm[device % N_MEM]
    position = jnp.arange(ROWS, dtype=jnp.int32)[None, :]
    other = (hot[:, None] + 1 + (position - CAP) % (N_GRP - 1)) % N_GRP
    pool = jnp.where(position < CAP, hot[:, None], other)
    hot_local = jax.random.randint(jax.random.fold_in(key, 14), (N_MEM,), 0, CL_GRP)[device % N_MEM]
    spare = jax.random.randint(jax.random.fold_in(key, 15), (devices, ROWS), 0, CL_GRP - 1)
    offset = jax.random.randint(jax.random.fold_in(key, 16), (devices, 1), 0, CL_GRP)
    cyclic = ((position - CAP) // (N_GRP - 1) + offset) % CL_GRP
    second = (hot_local[:, None] + 1 + spare) % CL_GRP
    local_pool = jnp.where(position < KCAP, hot_local[:, None], jnp.where(position < CAP, second, cyclic))
    keys = jax.random.split(jax.random.fold_in(key, 12), devices)
    shuffle = jax.vmap(lambda k: jax.random.permutation(k, ROWS))(keys)
    group = jnp.take_along_axis(pool, shuffle, axis=1).reshape(NROWS)
    local = jnp.take_along_axis(local_pool, shuffle, axis=1).reshape(NROWS)
    return (local * N_GRP + group).astype(jnp.int32)


def draw_cluster_id(key, part):
    return assign_clusters(key)


def draw_codes(key, part):
    clusters = assign_clusters(key)
    centers = jax.random.normal(jax.random.fold_in(key, 21), (CLUSTERS, D), jnp.float32)
    spread = jnp.exp(jax.random.uniform(jax.random.fold_in(key, 22), (NROWS, 1), jnp.float32, jnp.log(0.3), jnp.log(1.5)))
    noise = jax.random.normal(jax.random.fold_in(key, 23), (NROWS, D), jnp.float32)
    return (centers[clusters] + spread * noise).astype(jnp.bfloat16)


def levels(rng, dims, cuts, smallest, high):
    gain, own = 1.0, jax.random.fold_in(rng, 6)
    for axis_at, blocks in cuts:
        draws = jnp.exp(jax.random.uniform(jax.random.fold_in(own, axis_at), (blocks,), jnp.float32, smallest / len(cuts), high / len(cuts)))
        gain = gain * jnp.repeat(draws, dims[axis_at] // blocks).reshape([-1 if axis == axis_at else 1 for axis in range(len(dims))])
    return gain


def setup_inputs(seed: int = 0) -> dict:
    seeds = jax.random.split(jax.random.key(seed), 4)
    codes = draw_codes(jax.random.fold_in(seeds[3], 71), 0)
    scales = jnp.clip(jnp.exp(math.log(2.0) - 2.3025851 * jax.random.uniform(seeds[1], (NROWS, D // BLOCK), jnp.float32) ** levels(seeds[1], (NROWS, D // BLOCK), ((0, 32),), -0.2, 0.2)), 0.2, 2.0)
    cluster_id = draw_cluster_id(jax.random.fold_in(seeds[3], 71), 0)
    return {"codes": codes, "scales": scales, "cluster_id": cluster_id}


def embed(codes, scales):
    nblk = scales.shape[1]
    rows = codes.shape[0]
    x = (codes.astype(jnp.float32).reshape(rows, nblk, D // nblk) * scales[:, :, None]).reshape(rows, D)
    inv = lax.rsqrt(lax.optimization_barrier(jnp.mean(x * x, axis=1, keepdims=True)) + 1e-06)
    return (x * inv).astype(jnp.bfloat16)

def reference(codes, scales, cluster_id):
    hi = lax.Precision.HIGHEST
    padg = N_GRP * N_MEM * CAP
    embedding_rows = embed(codes, scales)
    owner = (cluster_id % N_GRP).astype(jnp.int32)
    order = jnp.argsort(owner, stable=True).astype(jnp.int32)
    sorted_by_owner = owner[order]
    counts = lax.optimization_barrier(jnp.sum((owner[None, :] == jnp.arange(N_GRP, dtype=jnp.int32)[:, None]).astype(jnp.int32), axis=1)).astype(jnp.int32)
    starts = (jnp.cumsum(counts) - counts).astype(jnp.int32)
    e_pad = jnp.concatenate([embedding_rows[order], jnp.zeros((padg, D), jnp.bfloat16)], axis=0)
    t_pad = jnp.concatenate([cluster_id[order], jnp.full((padg,), -1, jnp.int32)], axis=0)
    index = jnp.arange(padg, dtype=jnp.int32)

    def one_group(group):
        start = starts[group].astype(jnp.int32)
        rows = lax.dynamic_slice_in_dim(e_pad, start, padg, 0).astype(jnp.float32)
        tags = lax.dynamic_slice_in_dim(t_pad, start, padg, 0)
        tags = jnp.where(index < counts[group], tags, -1)
        sims = jnp.dot(rows, rows.T, precision=hi) / D
        keep = (tags[:, None] == tags[None, :]) & (tags[:, None] >= 0) & (index[:, None] != index[None, :])
        weights = jnp.where(keep, jnp.exp(8.0 * (sims - 1.0)), jnp.float32(0.0))
        den = 1.0 + lax.optimization_barrier(jnp.sum(weights, axis=1))
        wround = weights.astype(jnp.bfloat16).astype(jnp.float32)
        num = rows + jnp.dot(wround, rows, precision=hi)
        return ((num / den[:, None]).astype(jnp.bfloat16), jnp.log(den).astype(jnp.bfloat16))
    smooth_all, mass_all = lax.map(one_group, jnp.arange(N_GRP, dtype=jnp.int32))
    local = (jnp.arange(NROWS, dtype=jnp.int32) - starts[sorted_by_owner]).astype(jnp.int32)
    smooth_sorted = smooth_all[sorted_by_owner, local]
    mass_sorted = mass_all[sorted_by_owner, local]
    smoothed = jnp.zeros((NROWS, D), jnp.bfloat16).at[order].set(smooth_sorted)
    dup_mass = jnp.zeros((NROWS,), jnp.bfloat16).at[order].set(mass_sorted)
    return (smoothed, dup_mass)
```

```python
import functools

import jax
import jax.numpy as jnp
from jax import lax
from jax.experimental import pallas as pl
from jax.experimental.pallas import tpu as pltpu
from jax.sharding import PartitionSpec as P

CAP = 40
LANES = 128
VMEM = pl.BlockSpec(memory_space=pltpu.VMEM)


def as_column(row):
    n = row.shape[1]
    same = lax.broadcasted_iota(jnp.int32, (n, n), 0) == lax.broadcasted_iota(jnp.int32, (n, n), 1)
    return jnp.sum(jnp.where(same, jnp.broadcast_to(row, (n, n)), 0.0), axis=1, keepdims=True)


def pack_kernel(groups, codes_ref, scales_ref, cluster_ref, select_ref, *out_refs):
    rows, width = codes_ref.shape
    nblk = scales_ref.shape[0]
    step = width // nblk
    scales = scales_ref[...].T
    parts = []
    total = None
    for b in range(nblk):
        x = codes_ref[:, b * step : (b + 1) * step].astype(jnp.float32) * scales[:, b : b + 1]
        parts.append(x)
        square = x * x
        total = square if total is None else total + square
    inv = lax.rsqrt(jnp.sum(total, axis=1, keepdims=True) / width + 1e-06)
    cluster = cluster_ref[...]
    owner = lax.rem(cluster, groups)
    step_row = lax.bitwise_xor(owner, lax.axis_index("grp"))
    step_f = step_row.astype(jnp.float32)
    step_col = as_column(step_f)
    before = lax.broadcasted_iota(jnp.int32, (rows, rows), 0) < lax.broadcasted_iota(
        jnp.int32, (rows, rows), 1
    )
    rank = jnp.sum(
        jnp.where(before & (step_col == step_f), 1.0, 0.0), axis=0, keepdims=True
    ).astype(jnp.int32)
    target = step_row * CAP + rank
    slots = groups * CAP
    hit = lax.broadcasted_iota(jnp.int32, (slots, rows), 0) == target
    select = jnp.where(hit, 1.0, 0.0).astype(jnp.bfloat16)
    select_ref[...] = select
    tags = jnp.sum(jnp.where(hit, cluster.astype(jnp.float32) + 1.0, 0.0), axis=1, keepdims=True) - 1.0
    tags = jnp.broadcast_to(tags, (slots, LANES)).astype(jnp.bfloat16)
    for s in range(groups):
        out_refs[s][:, width:] = tags[s * CAP : (s + 1) * CAP]
    for b in range(nblk):
        e = (parts[b] * inv).astype(jnp.bfloat16)
        packed = jnp.dot(select, e, preferred_element_type=jnp.float32).astype(jnp.bfloat16)
        for s in range(groups):
            out_refs[s][:, b * step : (b + 1) * step] = packed[s * CAP : (s + 1) * CAP]


def smooth_kernel(groups, pieces, *refs):
    in_refs, out_refs, keys = refs[:pieces], refs[pieces : pieces + groups], refs[-1]
    width = in_refs[0].shape[1] - LANES
    for p in range(pieces):
        keys[p * CAP : (p + 1) * CAP, :] = in_refs[p][...]
    slots, count = groups * CAP, pieces * CAP
    queries = keys[:slots, :width]
    first = jnp.where(lax.broadcasted_iota(jnp.int32, (8, LANES), 1) == 0, 1.0, 0.0).astype(jnp.bfloat16)
    ktags = lax.dot_general(
        first, keys[:, width:], (((1,), (1,)), ((), ())), preferred_element_type=jnp.float32
    )[:1]
    qtags = keys[:slots, width : width + 1].astype(jnp.float32)
    sims = (
        lax.dot_general(
            queries, keys[:, :width], (((1,), (1,)), ((), ())), preferred_element_type=jnp.float32
        )
        / width
    )
    keep = (
        (qtags == ktags)
        & (qtags >= 0.0)
        & (
            lax.broadcasted_iota(jnp.int32, (slots, count), 0)
            != lax.broadcasted_iota(jnp.int32, (slots, count), 1)
        )
    )
    weights = jnp.where(keep, jnp.exp(8.0 * (sims - 1.0)), 0.0)
    den = 1.0 + jnp.sum(weights, axis=1, keepdims=True)
    num = jnp.dot(
        weights.astype(jnp.bfloat16), keys[:, :width], preferred_element_type=jnp.float32
    )
    result = ((queries.astype(jnp.float32) + num) / den).astype(jnp.bfloat16)
    mass = jnp.broadcast_to(jnp.log(den), (slots, LANES)).astype(jnp.bfloat16)
    for s in range(groups):
        out_refs[s][:, :width] = result[s * CAP : (s + 1) * CAP]
        out_refs[s][:, width:] = mass[s * CAP : (s + 1) * CAP]


def unpack_kernel(groups, select_ref, *refs):
    in_refs, (smoothed_ref, mass_ref, back) = refs[:groups], refs[groups:]
    width = smoothed_ref.shape[1]
    for s in range(groups):
        back[s * CAP : (s + 1) * CAP, :] = in_refs[s][...]
    select = select_ref[...]
    over_slots = (((0,), (0,)), ((), ()))
    smoothed_ref[...] = lax.dot_general(
        select, back[:, :width], over_slots, preferred_element_type=jnp.float32
    ).astype(jnp.bfloat16)
    mass_ref[...] = lax.dot_general(
        back[:, width:], select, over_slots, preferred_element_type=jnp.float32
    )[:1].astype(jnp.bfloat16)


def local(codes, scales, cluster_id):
    rows, width = codes.shape
    groups, members = lax.axis_size("grp"), lax.axis_size("mem")
    slots = groups * CAP
    piece = jax.ShapeDtypeStruct((CAP, width + LANES), jnp.bfloat16)

    def swap(value, axis, step):
        size = lax.axis_size(axis)
        return lax.ppermute(value, axis, [(i, i ^ step) for i in range(size)])

    select, *outbox = pl.pallas_call(
        functools.partial(pack_kernel, groups),
        out_shape=[jax.ShapeDtypeStruct((slots, rows), jnp.bfloat16)] + [piece] * groups,
        in_specs=[VMEM] * 3,
        out_specs=[VMEM] * (1 + groups),
        name="pack",
    )(codes, scales.T, cluster_id.reshape(1, rows))
    inbox = [outbox[0]] + [swap(outbox[s], "grp", s) for s in range(1, groups)]
    held = list(inbox)
    for step in range(2, members, 2):
        held += [swap(p, "mem", step) for p in inbox]
    held += [swap(p, "mem", 1) for p in held]
    results = pl.pallas_call(
        functools.partial(smooth_kernel, groups, len(held)),
        out_shape=[piece] * groups,
        in_specs=[VMEM] * len(held),
        out_specs=[VMEM] * groups,
        scratch_shapes=[pltpu.VMEM((len(held) * CAP, width + LANES), jnp.bfloat16)],
        name="smooth",
    )(*held)
    back = [results[0]] + [swap(results[s], "grp", s) for s in range(1, groups)]
    smoothed, mass = pl.pallas_call(
        functools.partial(unpack_kernel, groups),
        out_shape=[
            jax.ShapeDtypeStruct((rows, width), jnp.bfloat16),
            jax.ShapeDtypeStruct((1, rows), jnp.bfloat16),
        ],
        in_specs=[VMEM] * (1 + groups),
        out_specs=[VMEM] * 2,
        scratch_shapes=[pltpu.VMEM((slots, width + LANES), jnp.bfloat16)],
        name="unpack",
    )(select, *back)
    return (smoothed, mass.reshape(rows))


def solution(mesh):
    placed = (P(("grp", "mem"), None), P(("grp", "mem"), None), P(("grp", "mem")))
    return jax.shard_map(
        local,
        mesh=mesh,
        in_specs=placed,
        out_specs=(P(("grp", "mem"), None), P(("grp", "mem"))),
        check_vma=False,
    )
```

```python
import functools

import jax
import jax.numpy as jnp
from jax import lax
from jax.experimental import pallas as pl
from jax.experimental.pallas import tpu as pltpu
from jax.sharding import PartitionSpec as P

CAP = 40
LANES = 128
VMEM = pl.BlockSpec(memory_space=pltpu.VMEM)
ROOM = pltpu.CompilerParams(vmem_limit_bytes=24 * 2**20)


def as_column(row):
    n = row.shape[1]
    same = lax.broadcasted_iota(jnp.int32, (n, n), 0) == lax.broadcasted_iota(jnp.int32, (n, n), 1)
    return jnp.sum(jnp.where(same, jnp.broadcast_to(row, (n, n)), 0.0), axis=1, keepdims=True)


def slot_mask(slots):
    row = lax.broadcasted_iota(jnp.int32, (slots, LANES), 0)
    return lax.rem(row, CAP) == lax.broadcasted_iota(jnp.int32, (slots, LANES), 1)


def spread(rows_of_pieces, pieces):
    slots = pieces * CAP
    owner = lax.div(lax.broadcasted_iota(jnp.int32, (slots, pieces), 0), CAP)
    pick = jnp.where(owner == lax.broadcasted_iota(jnp.int32, (slots, pieces), 1), 1.0, 0.0)
    wide = jnp.dot(
        pick.astype(jnp.bfloat16), rows_of_pieces.astype(jnp.bfloat16), preferred_element_type=jnp.float32
    )
    return jnp.where(slot_mask(slots), wide, 0.0)


def gather_lanes(column, pieces):
    wide = jnp.where(slot_mask(pieces * CAP), column, 0.0)
    return [jnp.sum(wide[p * CAP : (p + 1) * CAP], axis=0, keepdims=True) for p in range(pieces)]


def pack_kernel(groups, codes_ref, scales_ref, cluster_ref, select_ref, *out_refs):
    rows, width = codes_ref.shape
    nblk = scales_ref.shape[0]
    step = width // nblk
    scales = scales_ref[...].T
    parts = []
    total = None
    for b in range(nblk):
        x = codes_ref[:, b * step : (b + 1) * step].astype(jnp.float32) * scales[:, b : b + 1]
        parts.append(x)
        square = x * x
        total = square if total is None else total + square
    inv = lax.rsqrt(jnp.sum(total, axis=1, keepdims=True) / width + 1e-06)
    cluster = cluster_ref[...]
    owner = lax.rem(cluster, groups)
    step_row = lax.bitwise_xor(owner, lax.axis_index("grp"))
    step_f = step_row.astype(jnp.float32)
    step_col = as_column(step_f)
    before = lax.broadcasted_iota(jnp.int32, (rows, rows), 0) < lax.broadcasted_iota(
        jnp.int32, (rows, rows), 1
    )
    rank = jnp.sum(
        jnp.where(before & (step_col == step_f), 1.0, 0.0), axis=0, keepdims=True
    ).astype(jnp.int32)
    target = step_row * CAP + rank
    slots = groups * CAP
    hit = lax.broadcasted_iota(jnp.int32, (slots, rows), 0) == target
    select = jnp.where(hit, 1.0, 0.0).astype(jnp.bfloat16)
    select_ref[...] = select
    tags = jnp.sum(jnp.where(hit, cluster.astype(jnp.float32) + 1.0, 0.0), axis=1, keepdims=True)
    for s, tag_row in enumerate(gather_lanes(tags, groups)):
        out_refs[s][nblk * CAP :, :] = jnp.broadcast_to(tag_row - 1.0, (8, LANES)).astype(jnp.bfloat16)
    for b in range(nblk):
        e = (parts[b] * inv).astype(jnp.bfloat16)
        packed = jnp.dot(select, e, preferred_element_type=jnp.float32).astype(jnp.bfloat16)
        for s in range(groups):
            out_refs[s][b * CAP : (b + 1) * CAP, :] = packed[s * CAP : (s + 1) * CAP]


def smooth_kernel(groups, places, nblk, *refs):
    inputs, pieces = len(places), groups * lax.axis_size("mem")
    in_refs, out_refs = refs[:inputs], refs[inputs : inputs + groups]
    keys_ref, tags_ref = refs[inputs + groups :]
    size = nblk * CAP + 8
    width = nblk * LANES
    for ref, blocks in zip(in_refs, places):
        for k, p in enumerate(blocks):
            if p is None:
                continue
            at = k * size
            for b in range(nblk):
                keys_ref[b, p * CAP : (p + 1) * CAP, :] = ref[at + b * CAP : at + (b + 1) * CAP, :]
            tags_ref[p : p + 1, :] = ref[at + nblk * CAP : at + nblk * CAP + 1, :].astype(jnp.float32)
    slots, count = groups * CAP, pieces * CAP
    keys = jnp.concatenate([keys_ref[b] for b in range(nblk)], axis=1)
    queries = keys[:slots]
    tags = spread(tags_ref[...], pieces)
    ktags = lax.dot_general(
        jnp.ones((8, LANES), jnp.bfloat16),
        tags.astype(jnp.bfloat16),
        (((1,), (1,)), ((), ())),
        preferred_element_type=jnp.float32,
    )[:1]
    qtags = jnp.sum(tags[:slots], axis=1, keepdims=True)
    sims = (
        lax.dot_general(
            queries, keys, (((1,), (1,)), ((), ())), preferred_element_type=jnp.float32
        )
        / width
    )
    keep = (
        (qtags == ktags)
        & (qtags >= 0.0)
        & (
            lax.broadcasted_iota(jnp.int32, (slots, count), 0)
            != lax.broadcasted_iota(jnp.int32, (slots, count), 1)
        )
    )
    weights = jnp.where(keep, jnp.exp(8.0 * (sims - 1.0)), 0.0)
    den = 1.0 + jnp.sum(weights, axis=1, keepdims=True)
    num = jnp.dot(weights.astype(jnp.bfloat16), keys, preferred_element_type=jnp.float32)
    result = ((queries.astype(jnp.float32) + num) / den).astype(jnp.bfloat16)
    for s, mass_row in enumerate(gather_lanes(jnp.log(den), groups)):
        for b in range(nblk):
            out_refs[s][b * CAP : (b + 1) * CAP, :] = result[
                s * CAP : (s + 1) * CAP, b * LANES : (b + 1) * LANES
            ]
        out_refs[s][nblk * CAP :, :] = jnp.broadcast_to(mass_row, (8, LANES)).astype(jnp.bfloat16)


def unpack_kernel(steps, nblk, select_ref, *refs):
    groups = len(steps)
    in_refs, (smoothed_ref, mass_ref, back_ref, masses_ref) = refs[:groups], refs[groups:]
    for s, ref in zip(steps, in_refs):
        for b in range(nblk):
            back_ref[b, s * CAP : (s + 1) * CAP, :] = ref[b * CAP : (b + 1) * CAP, :]
        masses_ref[s : s + 1, :] = ref[nblk * CAP : nblk * CAP + 1, :].astype(jnp.float32)
    select = select_ref[...]
    over_slots = (((0,), (0,)), ((), ()))
    back = jnp.concatenate([back_ref[b] for b in range(nblk)], axis=1)
    smoothed_ref[...] = lax.dot_general(
        select, back, over_slots, preferred_element_type=jnp.float32
    ).astype(jnp.bfloat16)
    masses = spread(masses_ref[...], groups).astype(jnp.bfloat16)
    mass = lax.dot_general(masses, select, over_slots, preferred_element_type=jnp.float32)
    mass_ref[...] = jnp.sum(mass, axis=0, keepdims=True).astype(jnp.bfloat16)


def gate(value, *after):
    if not after:
        return value
    return lax.optimization_barrier((value, *after))[0]


def on_chip(values):
    return [pltpu.with_memory_space_constraint(v, pltpu.VMEM) for v in values]


def local(codes, scales, cluster_id):
    rows, width = codes.shape
    nblk = scales.shape[1]
    groups, members = lax.axis_size("grp"), lax.axis_size("mem")
    slots = groups * CAP
    size = nblk * CAP + 8
    piece = pltpu.VMEM((size, LANES), jnp.bfloat16)
    half, sides = groups // 2, members // 2
    near, far = list(range(1, half)), list(range(half, groups))

    def swap(value, axis, step):
        count = lax.axis_size(axis)
        return lax.ppermute(value, axis, [(i, i ^ step) for i in range(count)])

    def join(values):
        return jnp.concatenate(values) if len(values) > 1 else values[0]

    select, *outbox = pl.pallas_call(
        functools.partial(pack_kernel, groups),
        out_shape=[pltpu.VMEM((slots, rows), jnp.bfloat16)] + [piece] * groups,
        in_specs=[VMEM] * 3,
        out_specs=[VMEM] * (1 + groups),
        compiler_params=ROOM,
        name="pack",
    )(codes, scales.T, cluster_id.reshape(1, rows))

    held = []

    def hold(value, where):
        held.append((value, where))
        return held[-1]

    def across(parts, *after):
        joined = gate(join([v for v, _ in parts]), *after)
        where = [w for _, ws in parts for w in ws]
        return [
            (swap(joined, "mem", step), [(s, step // 2) for s, _ in where]) for step in range(2, members, 2)
        ], joined

    def partner(parts, *after):
        joined = gate(join([v for v, _ in parts]), *after)
        return (swap(joined, "mem", 1), [(s, i + sides) for _, ws in parts for s, i in ws])

    def grp(s, *after):
        return (swap(gate(outbox[s], *after), "grp", s), [(s, 0)])

    early, late = far[: half // 2], far[half // 2 :]
    got = {0: (outbox[0], [(0, 0)])}
    for s in early[:1] + near + early[1:]:
        got[s] = grp(s)
    ready = [got[s] for s in [0] + near]
    first, joined = across(ready)
    for s in late:
        got[s] = grp(s, joined)
    second, _ = across([got[s] for s in early])
    third, last = across([got[s] for s in late])
    held = [got[s] for s in early[:1] + near + early[1:] + late] + first + second + third + [got[0]]
    held += [partner(ready + [got[s] for s in early]), partner(first)]
    held += [partner([got[s] for s in late] + second)]
    held += [partner([h]) for h in third]

    steps = [s for pair in zip(far, near + [0]) for s in pair]
    places = [[i * groups + steps.index(s) for s, i in where] for _, where in held]
    pieces = groups * members
    results = pl.pallas_call(
        functools.partial(smooth_kernel, groups, places, nblk),
        out_shape=[piece] * groups,
        in_specs=[VMEM] * len(held),
        out_specs=[VMEM] * groups,
        scratch_shapes=[
            pltpu.VMEM((nblk, pieces * CAP, LANES), jnp.bfloat16),
            pltpu.VMEM((pieces, LANES), jnp.float32),
        ],
        compiler_params=ROOM,
        name="smooth",
    )(*on_chip([v for v, _ in held]))
    result = dict(zip(steps, results))
    back = {s: swap(result[s], "grp", s) if s else result[s] for s in steps}
    done = steps
    smoothed, mass = pl.pallas_call(
        functools.partial(unpack_kernel, done, nblk),
        out_shape=[
            jax.ShapeDtypeStruct((rows, width), jnp.bfloat16),
            jax.ShapeDtypeStruct((1, rows), jnp.bfloat16),
        ],
        in_specs=[VMEM] * (1 + groups),
        out_specs=[VMEM] * 2,
        scratch_shapes=[
            pltpu.VMEM((nblk, slots, LANES), jnp.bfloat16),
            pltpu.VMEM((groups, LANES), jnp.float32),
        ],
        compiler_params=ROOM,
        name="unpack",
    )(*on_chip([select] + [back[s] for s in done]))
    return (smoothed, mass.reshape(rows))


def solution(mesh):
    placed = (P(("grp", "mem"), None), P(("grp", "mem"), None), P(("grp", "mem")))
    return jax.shard_map(
        local,
        mesh=mesh,
        in_specs=placed,
        out_specs=(P(("grp", "mem"), None), P(("grp", "mem"))),
        check_vma=False,
    )
```

```python
import functools

import jax
import jax.numpy as jnp
from jax import lax
from jax.experimental import pallas as pl
from jax.experimental.pallas import tpu as pltpu
from jax.sharding import PartitionSpec as P

CAP = 40
LANES = 128
VMEM = pl.BlockSpec(memory_space=pltpu.VMEM)
HBM = pl.BlockSpec(memory_space=pltpu.HBM)
ROOM = pltpu.CompilerParams(vmem_limit_bytes=24 * 2**20)


def as_column(row):
    n = row.shape[1]
    same = lax.broadcasted_iota(jnp.int32, (n, n), 0) == lax.broadcasted_iota(jnp.int32, (n, n), 1)
    return jnp.sum(jnp.where(same, jnp.broadcast_to(row, (n, n)), 0.0), axis=1, keepdims=True)


def slot_mask(slots):
    row = lax.broadcasted_iota(jnp.int32, (slots, LANES), 0)
    return lax.rem(row, CAP) == lax.broadcasted_iota(jnp.int32, (slots, LANES), 1)


def spread(rows_of_pieces, pieces):
    slots = pieces * CAP
    owner = lax.div(lax.broadcasted_iota(jnp.int32, (slots, pieces), 0), CAP)
    pick = jnp.where(owner == lax.broadcasted_iota(jnp.int32, (slots, pieces), 1), 1.0, 0.0)
    wide = jnp.dot(
        pick.astype(jnp.bfloat16), rows_of_pieces.astype(jnp.bfloat16), preferred_element_type=jnp.float32
    )
    return jnp.where(slot_mask(slots), wide, 0.0)


def gather_lanes(column, pieces):
    wide = jnp.where(slot_mask(pieces * CAP), column, 0.0)
    return [jnp.sum(wide[p * CAP : (p + 1) * CAP], axis=0, keepdims=True) for p in range(pieces)]


def pack_kernel(groups, codes_hbm, scales_hbm, cluster_hbm, select_ref, *refs):
    out_refs, (codes_ref, scales_ref, cluster_ref, sems) = refs[:groups], refs[groups:]
    copies = [
        pltpu.make_async_copy(src, dst, sems.at[i])
        for i, (src, dst) in enumerate(
            ((cluster_hbm, cluster_ref), (scales_hbm, scales_ref), (codes_hbm, codes_ref))
        )
    ]
    for copy in copies:
        copy.start()
    rows, width = codes_ref.shape
    nblk = scales_ref.shape[0]
    step = width // nblk
    copies[0].wait()
    cluster = cluster_ref[...]
    owner = lax.rem(cluster, groups)
    step_row = lax.bitwise_xor(owner, lax.axis_index("grp"))
    step_f = step_row.astype(jnp.float32)
    step_col = as_column(step_f)
    before = lax.broadcasted_iota(jnp.int32, (rows, rows), 0) < lax.broadcasted_iota(
        jnp.int32, (rows, rows), 1
    )
    rank = jnp.sum(
        jnp.where(before & (step_col == step_f), 1.0, 0.0), axis=0, keepdims=True
    ).astype(jnp.int32)
    target = step_row * CAP + rank
    slots = groups * CAP
    hit = lax.broadcasted_iota(jnp.int32, (slots, rows), 0) == target
    select = jnp.where(hit, 1.0, 0.0).astype(jnp.bfloat16)
    select_ref[...] = select
    tags = jnp.sum(jnp.where(hit, cluster.astype(jnp.float32) + 1.0, 0.0), axis=1, keepdims=True)
    for s, tag_row in enumerate(gather_lanes(tags, groups)):
        out_refs[s][nblk * CAP :, :] = jnp.broadcast_to(tag_row - 1.0, (8, LANES)).astype(jnp.bfloat16)
    copies[1].wait()
    copies[2].wait()
    scales = scales_ref[...].T
    parts = []
    total = None
    for b in range(nblk):
        x = codes_ref[:, b * step : (b + 1) * step].astype(jnp.float32) * scales[:, b : b + 1]
        parts.append(x)
        square = x * x
        total = square if total is None else total + square
    inv = lax.rsqrt(jnp.sum(total, axis=1, keepdims=True) / width + 1e-06)
    for b in range(nblk):
        e = (parts[b] * inv).astype(jnp.bfloat16)
        packed = jnp.dot(select, e, preferred_element_type=jnp.float32).astype(jnp.bfloat16)
        for s in range(groups):
            out_refs[s][b * CAP : (b + 1) * CAP, :] = packed[s * CAP : (s + 1) * CAP]


def smooth_kernel(groups, places, nblk, *refs):
    inputs, pieces = len(places), groups * lax.axis_size("mem")
    in_refs, out_refs = refs[:inputs], refs[inputs : inputs + groups]
    keys_ref, tags_ref = refs[inputs + groups :]
    size = nblk * CAP + 8
    width = nblk * LANES
    for ref, blocks in zip(in_refs, places):
        for k, p in enumerate(blocks):
            if p is None:
                continue
            at = k * size
            for b in range(nblk):
                keys_ref[b, p * CAP : (p + 1) * CAP, :] = ref[at + b * CAP : at + (b + 1) * CAP, :]
            tags_ref[p : p + 1, :] = ref[at + nblk * CAP : at + nblk * CAP + 1, :].astype(jnp.float32)
    slots, count = groups * CAP, pieces * CAP
    keys = jnp.concatenate([keys_ref[b] for b in range(nblk)], axis=1)
    queries = keys[:slots]
    tags = spread(tags_ref[...], pieces)
    ktags = lax.dot_general(
        jnp.ones((8, LANES), jnp.bfloat16),
        tags.astype(jnp.bfloat16),
        (((1,), (1,)), ((), ())),
        preferred_element_type=jnp.float32,
    )[:1]
    qtags = jnp.sum(tags[:slots], axis=1, keepdims=True)
    sims = (
        lax.dot_general(
            queries, keys, (((1,), (1,)), ((), ())), preferred_element_type=jnp.float32
        )
        / width
    )
    keep = (
        (qtags == ktags)
        & (qtags >= 0.0)
        & (
            lax.broadcasted_iota(jnp.int32, (slots, count), 0)
            != lax.broadcasted_iota(jnp.int32, (slots, count), 1)
        )
    )
    weights = jnp.where(keep, jnp.exp(8.0 * (sims - 1.0)), 0.0)
    den = 1.0 + jnp.sum(weights, axis=1, keepdims=True)
    num = jnp.dot(weights.astype(jnp.bfloat16), keys, preferred_element_type=jnp.float32)
    result = ((queries.astype(jnp.float32) + num) / den).astype(jnp.bfloat16)
    for s, mass_row in enumerate(gather_lanes(jnp.log(den), groups)):
        for b in range(nblk):
            out_refs[s][b * CAP : (b + 1) * CAP, :] = result[
                s * CAP : (s + 1) * CAP, b * LANES : (b + 1) * LANES
            ]
        out_refs[s][nblk * CAP :, :] = jnp.broadcast_to(mass_row, (8, LANES)).astype(jnp.bfloat16)


def unpack_kernel(steps, nblk, select_ref, *refs):
    groups = len(steps)
    in_refs, (smoothed_ref, mass_ref, back_ref, masses_ref) = refs[:groups], refs[groups:]
    for s, ref in zip(steps, in_refs):
        for b in range(nblk):
            back_ref[b, s * CAP : (s + 1) * CAP, :] = ref[b * CAP : (b + 1) * CAP, :]
        masses_ref[s : s + 1, :] = ref[nblk * CAP : nblk * CAP + 1, :].astype(jnp.float32)
    select = select_ref[...]
    over_slots = (((0,), (0,)), ((), ()))
    back = jnp.concatenate([back_ref[b] for b in range(nblk)], axis=1)
    smoothed_ref[...] = lax.dot_general(
        select, back, over_slots, preferred_element_type=jnp.float32
    ).astype(jnp.bfloat16)
    masses = spread(masses_ref[...], groups).astype(jnp.bfloat16)
    mass = lax.dot_general(masses, select, over_slots, preferred_element_type=jnp.float32)
    mass_ref[...] = jnp.sum(mass, axis=0).astype(jnp.bfloat16)


def gate(value, *after):
    if not after:
        return value
    return lax.optimization_barrier((value, *after))[0]


def off_chip(values):
    return [pltpu.with_memory_space_constraint(v, pltpu.HBM) for v in values]


def on_chip(values):
    return [pltpu.with_memory_space_constraint(v, pltpu.VMEM) for v in values]


def local(codes, scales, cluster_id):
    rows, width = codes.shape
    nblk = scales.shape[1]
    groups, members = lax.axis_size("grp"), lax.axis_size("mem")
    slots = groups * CAP
    size = nblk * CAP + 8
    piece = pltpu.VMEM((size, LANES), jnp.bfloat16)
    half, sides = groups // 2, members // 2
    near, far = list(range(1, half)), list(range(half, groups))

    def swap(value, axis, step):
        count = lax.axis_size(axis)
        return lax.ppermute(value, axis, [(i, i ^ step) for i in range(count)])

    def join(values):
        return jnp.concatenate(values) if len(values) > 1 else values[0]

    select, *outbox = pl.pallas_call(
        functools.partial(pack_kernel, groups),
        out_shape=[pltpu.VMEM((slots, rows), jnp.bfloat16)] + [piece] * groups,
        in_specs=[HBM] * 3,
        out_specs=[VMEM] * (1 + groups),
        scratch_shapes=[
            pltpu.VMEM(codes.shape, codes.dtype),
            pltpu.VMEM((nblk, rows), scales.dtype),
            pltpu.VMEM((1, rows), cluster_id.dtype),
            pltpu.SemaphoreType.DMA((3,)),
        ],
        compiler_params=ROOM,
        name="pack",
    )(*off_chip([codes, scales.T, cluster_id.reshape(1, rows)]))

    held = []

    def hold(value, where):
        held.append((value, where))
        return held[-1]

    def across(parts, *after):
        joined = gate(join([v for v, _ in parts]), *after)
        where = [w for _, ws in parts for w in ws]
        return [
            (swap(joined, "mem", step), [(s, step // 2) for s, _ in where]) for step in range(2, members, 2)
        ], joined

    def partner(parts, *after):
        joined = gate(join([v for v, _ in parts]), *after)
        return (swap(joined, "mem", 1), [(s, i + sides) for _, ws in parts for s, i in ws])

    def grp(s, *after):
        return (swap(gate(outbox[s], *after), "grp", s), [(s, 0)])

    got = {0: (outbox[0], [(0, 0)])}
    early, late = far[: half // 2], far[half // 2 :]
    for s in early[:1] + [1] + near[1:2] + early[1:]:
        got[s] = grp(s)
    ready = [got[0], got[1]]
    first, joined = across(ready)
    for s in near[2:] + late:
        got[s] = grp(s, joined)
    mid = [got[s] for s in near[1:] + early]
    second, _ = across(mid, joined)
    third, last = across([got[s] for s in late])
    held = [got[s] for s in early[:1] + [1] + near[1:2] + early[1:] + near[2:] + late] + first + second + third + [got[0]]
    held += [partner(ready + mid[:1]), partner(mid[1:]), partner(first)]
    held += [partner([got[s] for s in late])]
    held += [partner([h]) for h in second + third]
    steps = [s for pair in zip(far, near + [0]) for s in pair]
    places = [[i * groups + steps.index(s) for s, i in where] for _, where in held]
    pieces = groups * members
    results = pl.pallas_call(
        functools.partial(smooth_kernel, groups, places, nblk),
        out_shape=[piece] * groups,
        in_specs=[VMEM] * len(held),
        out_specs=[VMEM] * groups,
        scratch_shapes=[
            pltpu.VMEM((nblk, pieces * CAP, LANES), jnp.bfloat16),
            pltpu.VMEM((pieces, LANES), jnp.float32),
        ],
        compiler_params=ROOM,
        name="smooth",
    )(*on_chip([v for v, _ in held]))
    result = dict(zip(steps, results))
    back = {s: swap(result[s], "grp", s) if s else result[s] for s in steps}
    done = steps
    smoothed, mass = pl.pallas_call(
        functools.partial(unpack_kernel, done, nblk),
        out_shape=[
            jax.ShapeDtypeStruct((rows, width), jnp.bfloat16),
            jax.ShapeDtypeStruct((rows,), jnp.bfloat16),
        ],
        in_specs=[VMEM] * (1 + groups),
        out_specs=[VMEM] * 2,
        scratch_shapes=[
            pltpu.VMEM((nblk, slots, LANES), jnp.bfloat16),
            pltpu.VMEM((groups, LANES), jnp.float32),
        ],
        compiler_params=ROOM,
        name="unpack",
    )(*on_chip([select] + [back[s] for s in done]))
    return (smoothed, mass)


def solution(mesh):
    placed = (P(("grp", "mem"), None), P(("grp", "mem"), None), P(("grp", "mem")))
    return jax.shard_map(
        local,
        mesh=mesh,
        in_specs=placed,
        out_specs=(P(("grp", "mem"), None), P(("grp", "mem"))),
        check_vma=False,
    )
```

```python
import functools

import jax
import jax.numpy as jnp
from jax import lax
from jax.experimental import pallas as pl
from jax.experimental.pallas import tpu as pltpu
from jax.sharding import PartitionSpec as P

CAP = 40
LANES = 128
VMEM = pl.BlockSpec(memory_space=pltpu.VMEM)
HBM = pl.BlockSpec(memory_space=pltpu.HBM)
ROOM = pltpu.CompilerParams(vmem_limit_bytes=24 * 2**20)


def as_column(row):
    n = row.shape[1]
    same = lax.broadcasted_iota(jnp.int32, (n, n), 0) == lax.broadcasted_iota(jnp.int32, (n, n), 1)
    return jnp.sum(jnp.where(same, jnp.broadcast_to(row, (n, n)), 0.0), axis=1, keepdims=True)


def slot_mask(slots):
    row = lax.broadcasted_iota(jnp.int32, (slots, LANES), 0)
    return lax.rem(row, CAP) == lax.broadcasted_iota(jnp.int32, (slots, LANES), 1)


def spread(rows_of_pieces, pieces):
    slots = pieces * CAP
    owner = lax.div(lax.broadcasted_iota(jnp.int32, (slots, pieces), 0), CAP)
    pick = jnp.where(owner == lax.broadcasted_iota(jnp.int32, (slots, pieces), 1), 1.0, 0.0)
    wide = jnp.dot(
        pick.astype(jnp.bfloat16), rows_of_pieces.astype(jnp.bfloat16), preferred_element_type=jnp.float32
    )
    return jnp.where(slot_mask(slots), wide, 0.0)


def gather_lanes(column, pieces):
    wide = jnp.where(slot_mask(pieces * CAP), column, 0.0)
    return [jnp.sum(wide[p * CAP : (p + 1) * CAP], axis=0, keepdims=True) for p in range(pieces)]


def pack_kernel(groups, codes_hbm, scales_hbm, cluster_hbm, select_ref, *refs):
    out_refs, (codes_ref, scales_ref, cluster_ref, sems) = refs[:groups], refs[groups:]
    copies = [
        pltpu.make_async_copy(src, dst, sems.at[i])
        for i, (src, dst) in enumerate(
            ((cluster_hbm, cluster_ref), (scales_hbm, scales_ref), (codes_hbm, codes_ref))
        )
    ]
    for copy in copies:
        copy.start()
    rows, width = codes_ref.shape
    nblk = scales_ref.shape[0]
    step = width // nblk
    copies[0].wait()
    cluster = cluster_ref[...]
    owner = lax.rem(cluster, groups)
    step_row = lax.bitwise_xor(owner, lax.axis_index("grp"))
    step_f = step_row.astype(jnp.float32)
    step_col = as_column(step_f)
    before = lax.broadcasted_iota(jnp.int32, (rows, rows), 0) < lax.broadcasted_iota(
        jnp.int32, (rows, rows), 1
    )
    rank = jnp.sum(
        jnp.where(before & (step_col == step_f), 1.0, 0.0), axis=0, keepdims=True
    ).astype(jnp.int32)
    target = step_row * CAP + rank
    slots = groups * CAP
    hit = lax.broadcasted_iota(jnp.int32, (slots, rows), 0) == target
    select = jnp.where(hit, 1.0, 0.0).astype(jnp.bfloat16)
    select_ref[...] = select
    tags = jnp.sum(jnp.where(hit, cluster.astype(jnp.float32) + 1.0, 0.0), axis=1, keepdims=True)
    for s, tag_row in enumerate(gather_lanes(tags, groups)):
        out_refs[s][nblk * CAP :, :] = jnp.broadcast_to(tag_row - 1.0, (8, LANES)).astype(jnp.bfloat16)
    copies[1].wait()
    copies[2].wait()
    scales = scales_ref[...].T
    parts = []
    total = None
    for b in range(nblk):
        x = codes_ref[:, b * step : (b + 1) * step].astype(jnp.float32) * scales[:, b : b + 1]
        parts.append(x)
        square = x * x
        total = square if total is None else total + square
    inv = lax.rsqrt(jnp.sum(total, axis=1, keepdims=True) / width + 1e-06)
    for at in range(0, nblk, 8):
        e = jnp.concatenate([(x * inv).astype(jnp.bfloat16) for x in parts[at : at + 8]], axis=1)
        packed = jnp.dot(select, e, preferred_element_type=jnp.float32).astype(jnp.bfloat16)
        for k in range(e.shape[1] // step):
            b = at + k
            for s in range(groups):
                out_refs[s][b * CAP : (b + 1) * CAP, :] = packed[
                    s * CAP : (s + 1) * CAP, k * step : (k + 1) * step
                ]


def smooth_kernel(groups, places, nblk, *refs):
    inputs, pieces = len(places), groups * lax.axis_size("mem")
    in_refs, out_refs = refs[:inputs], refs[inputs : inputs + groups]
    keys_ref, tags_ref = refs[inputs + groups :]
    size = nblk * CAP + 8
    width = nblk * LANES
    for ref, blocks in zip(in_refs, places):
        for k, p in enumerate(blocks):
            if p is None:
                continue
            at = k * size
            for b in range(nblk):
                keys_ref[b, p * CAP : (p + 1) * CAP, :] = ref[at + b * CAP : at + (b + 1) * CAP, :]
            tags_ref[p : p + 1, :] = ref[at + nblk * CAP : at + nblk * CAP + 1, :].astype(jnp.float32)
    slots, count = groups * CAP, pieces * CAP
    keys = jnp.concatenate([keys_ref[b] for b in range(nblk)], axis=1)
    queries = keys[:slots]
    tags = spread(tags_ref[...], pieces)
    ktags = lax.dot_general(
        jnp.ones((8, LANES), jnp.bfloat16),
        tags.astype(jnp.bfloat16),
        (((1,), (1,)), ((), ())),
        preferred_element_type=jnp.float32,
    )[:1]
    qtags = jnp.sum(tags[:slots], axis=1, keepdims=True)
    sims = (
        lax.dot_general(
            queries, keys, (((1,), (1,)), ((), ())), preferred_element_type=jnp.float32
        )
    )
    keep = (
        (qtags == ktags)
        & (qtags >= 0.0)
        & (
            lax.broadcasted_iota(jnp.int32, (slots, count), 0)
            != lax.broadcasted_iota(jnp.int32, (slots, count), 1)
        )
    )
    weights = jnp.where(keep, jnp.exp(sims * (8.0 / width) - 8.0), 0.0)
    den = 1.0 + jnp.sum(weights, axis=1, keepdims=True)
    num = jnp.dot(weights.astype(jnp.bfloat16), keys, preferred_element_type=jnp.float32)
    result = ((queries.astype(jnp.float32) + num) * (1.0 / den)).astype(jnp.bfloat16)
    for s, mass_row in enumerate(gather_lanes(jnp.log(den), groups)):
        for b in range(nblk):
            out_refs[s][b * CAP : (b + 1) * CAP, :] = result[
                s * CAP : (s + 1) * CAP, b * LANES : (b + 1) * LANES
            ]
        out_refs[s][nblk * CAP :, :] = jnp.broadcast_to(mass_row, (8, LANES)).astype(jnp.bfloat16)


def unpack_kernel(steps, nblk, select_ref, *refs):
    groups = len(steps)
    in_refs, (smoothed_ref, mass_ref, back_ref, masses_ref) = refs[:groups], refs[groups:]
    for s, ref in zip(steps, in_refs):
        for b in range(nblk):
            back_ref[b, s * CAP : (s + 1) * CAP, :] = ref[b * CAP : (b + 1) * CAP, :]
        masses_ref[s : s + 1, :] = ref[nblk * CAP : nblk * CAP + 1, :].astype(jnp.float32)
    select = select_ref[...]
    over_slots = (((0,), (0,)), ((), ()))
    back = jnp.concatenate([back_ref[b] for b in range(nblk)], axis=1)
    smoothed_ref[...] = lax.dot_general(
        select, back, over_slots, preferred_element_type=jnp.float32
    ).astype(jnp.bfloat16)
    masses = spread(masses_ref[...], groups).astype(jnp.bfloat16)
    mass = lax.dot_general(masses, select, over_slots, preferred_element_type=jnp.float32)
    mass_ref[...] = jnp.sum(mass, axis=0).astype(jnp.bfloat16)


def gate(value, *after):
    if not after:
        return value
    return lax.optimization_barrier((value, *after))[0]


def off_chip(values):
    return [pltpu.with_memory_space_constraint(v, pltpu.HBM) for v in values]


def on_chip(values):
    return [pltpu.with_memory_space_constraint(v, pltpu.VMEM) for v in values]


def local(codes, scales, cluster_id):
    rows, width = codes.shape
    nblk = scales.shape[1]
    groups, members = lax.axis_size("grp"), lax.axis_size("mem")
    slots = groups * CAP
    size = nblk * CAP + 8
    piece = pltpu.VMEM((size, LANES), jnp.bfloat16)
    half, sides = groups // 2, members // 2
    near, far = list(range(1, half)), list(range(half, groups))

    def swap(value, axis, step):
        count = lax.axis_size(axis)
        return lax.ppermute(value, axis, [(i, i ^ step) for i in range(count)])

    def join(values):
        return jnp.concatenate(values) if len(values) > 1 else values[0]

    select, *outbox = pl.pallas_call(
        functools.partial(pack_kernel, groups),
        out_shape=[pltpu.VMEM((slots, rows), jnp.bfloat16)] + [piece] * groups,
        in_specs=[HBM] * 3,
        out_specs=[VMEM] * (1 + groups),
        scratch_shapes=[
            pltpu.VMEM(codes.shape, codes.dtype),
            pltpu.VMEM((nblk, rows), scales.dtype),
            pltpu.VMEM((1, rows), cluster_id.dtype),
            pltpu.SemaphoreType.DMA((3,)),
        ],
        compiler_params=ROOM,
        name="pack",
    )(*off_chip([codes, scales.T, cluster_id.reshape(1, rows)]))

    held = []

    def hold(value, where):
        held.append((value, where))
        return held[-1]

    def across(parts, *after):
        joined = gate(join([v for v, _ in parts]), *after)
        where = [w for _, ws in parts for w in ws]
        return [
            (swap(joined, "mem", step), [(s, step // 2) for s, _ in where]) for step in range(2, members, 2)
        ], joined

    def partner(parts, *after):
        joined = gate(join([v for v, _ in parts]), *after)
        return (swap(joined, "mem", 1), [(s, i + sides) for _, ws in parts for s, i in ws])

    def grp(s, *after):
        return (swap(gate(outbox[s], *after), "grp", s), [(s, 0)])

    got = {0: (outbox[0], [(0, 0)])}
    early, late = far[: half // 2], far[half // 2 :]
    for s in early[:1] + [1] + near[1:2] + early[1:]:
        got[s] = grp(s)
    ready = [got[0], got[1]]
    first, joined = across(ready)
    for s in near[2:] + late:
        got[s] = grp(s, joined)
    mid = [got[s] for s in near[1:] + early]
    second, _ = across(mid, joined)
    third, last = across([got[s] for s in late])
    held = [got[s] for s in early[:1] + [1] + near[1:2] + early[1:] + near[2:] + late] + first + second + third + [got[0]]
    held += [partner(ready + mid[:1]), partner(mid[1:]), partner(first)]
    held += [partner([got[s] for s in late])]
    held += [partner([h]) for h in second + third]
    steps = [s for pair in zip(far, near + [0]) for s in pair]
    places = [[i * groups + steps.index(s) for s, i in where] for _, where in held]
    pieces = groups * members
    results = pl.pallas_call(
        functools.partial(smooth_kernel, groups, places, nblk),
        out_shape=[piece] * groups,
        in_specs=[VMEM] * len(held),
        out_specs=[VMEM] * groups,
        scratch_shapes=[
            pltpu.VMEM((nblk, pieces * CAP, LANES), jnp.bfloat16),
            pltpu.VMEM((pieces, LANES), jnp.float32),
        ],
        compiler_params=ROOM,
        name="smooth",
    )(*on_chip([v for v, _ in held]))
    result = dict(zip(steps, results))
    back = {s: swap(result[s], "grp", s) if s else result[s] for s in steps}
    done = steps
    smoothed, mass = pl.pallas_call(
        functools.partial(unpack_kernel, done, nblk),
        out_shape=[
            jax.ShapeDtypeStruct((rows, width), jnp.bfloat16),
            jax.ShapeDtypeStruct((rows,), jnp.bfloat16),
        ],
        in_specs=[VMEM] * (1 + groups),
        out_specs=[VMEM] * 2,
        scratch_shapes=[
            pltpu.VMEM((nblk, slots, LANES), jnp.bfloat16),
            pltpu.VMEM((groups, LANES), jnp.float32),
        ],
        compiler_params=ROOM,
        name="unpack",
    )(*on_chip([select] + [back[s] for s in done]))
    return (smoothed, mass)


def solution(mesh):
    placed = (P(("grp", "mem"), None), P(("grp", "mem"), None), P(("grp", "mem")))
    return jax.shard_map(
        local,
        mesh=mesh,
        in_specs=placed,
        out_specs=(P(("grp", "mem"), None), P(("grp", "mem"))),
        check_vma=False,
    )
```

```python
import functools

import jax
import jax.numpy as jnp
from jax import lax
from jax.experimental import pallas as pl
from jax.experimental.pallas import tpu as pltpu
from jax.sharding import PartitionSpec as P

CAP = 40
LANES = 128
VMEM = pl.BlockSpec(memory_space=pltpu.VMEM)
HBM = pl.BlockSpec(memory_space=pltpu.HBM)
ROOM = pltpu.CompilerParams(vmem_limit_bytes=24 * 2**20)


def as_column(row):
    n = row.shape[1]
    same = lax.broadcasted_iota(jnp.int32, (n, n), 0) == lax.broadcasted_iota(jnp.int32, (n, n), 1)
    return jnp.sum(jnp.where(same, jnp.broadcast_to(row, (n, n)), 0.0), axis=1, keepdims=True)


def slot_mask(slots):
    row = lax.broadcasted_iota(jnp.int32, (slots, LANES), 0)
    return lax.rem(row, CAP) == lax.broadcasted_iota(jnp.int32, (slots, LANES), 1)


def spread(rows_of_pieces, pieces):
    slots = pieces * CAP
    owner = lax.div(lax.broadcasted_iota(jnp.int32, (slots, pieces), 0), CAP)
    pick = jnp.where(owner == lax.broadcasted_iota(jnp.int32, (slots, pieces), 1), 1.0, 0.0)
    wide = jnp.dot(
        pick.astype(jnp.bfloat16), rows_of_pieces.astype(jnp.bfloat16), preferred_element_type=jnp.float32
    )
    return jnp.where(slot_mask(slots), wide, 0.0)


def gather_lanes(column, pieces):
    wide = jnp.where(slot_mask(pieces * CAP), column, 0.0)
    return [jnp.sum(wide[p * CAP : (p + 1) * CAP], axis=0, keepdims=True) for p in range(pieces)]


def pack_kernel(groups, codes_hbm, scales_hbm, cluster_hbm, select_ref, *refs):
    out_refs, (codes_ref, scales_ref, cluster_ref, sems) = refs[:groups], refs[groups:]
    copies = [
        pltpu.make_async_copy(src, dst, sems.at[i])
        for i, (src, dst) in enumerate(
            ((cluster_hbm, cluster_ref), (scales_hbm, scales_ref), (codes_hbm, codes_ref))
        )
    ]
    for copy in copies:
        copy.start()
    rows, width = codes_ref.shape
    nblk = scales_ref.shape[0]
    step = width // nblk
    copies[0].wait()
    cluster = cluster_ref[...]
    owner = lax.rem(cluster, groups)
    step_row = lax.bitwise_xor(owner, lax.axis_index("grp"))
    step_f = step_row.astype(jnp.float32)
    step_col = as_column(step_f)
    before = lax.broadcasted_iota(jnp.int32, (rows, rows), 0) < lax.broadcasted_iota(
        jnp.int32, (rows, rows), 1
    )
    rank = jnp.sum(
        jnp.where(before & (step_col == step_f), 1.0, 0.0), axis=0, keepdims=True
    ).astype(jnp.int32)
    target = step_row * CAP + rank
    slots = groups * CAP
    hit = lax.broadcasted_iota(jnp.int32, (slots, rows), 0) == target
    select = jnp.where(hit, 1.0, 0.0).astype(jnp.bfloat16)
    select_ref[...] = select
    tags = jnp.sum(jnp.where(hit, cluster.astype(jnp.float32) + 1.0, 0.0), axis=1, keepdims=True)
    for s, tag_row in enumerate(gather_lanes(tags, groups)):
        out_refs[s][nblk * CAP :, :] = jnp.broadcast_to(tag_row - 1.0, (8, LANES)).astype(jnp.bfloat16)
    copies[1].wait()
    copies[2].wait()
    scales = scales_ref[...].T
    parts = []
    total = None
    for b in range(nblk):
        x = codes_ref[:, b * step : (b + 1) * step].astype(jnp.float32) * scales[:, b : b + 1]
        parts.append(x)
        square = x * x
        total = square if total is None else total + square
    inv = lax.rsqrt(jnp.sum(total, axis=1, keepdims=True) / width + 1e-06)
    for at in range(0, nblk, 8):
        e = jnp.concatenate([(x * inv).astype(jnp.bfloat16) for x in parts[at : at + 8]], axis=1)
        packed = jnp.dot(select, e, preferred_element_type=jnp.float32).astype(jnp.bfloat16)
        for k in range(e.shape[1] // step):
            b = at + k
            for s in range(groups):
                out_refs[s][b * CAP : (b + 1) * CAP, :] = packed[
                    s * CAP : (s + 1) * CAP, k * step : (k + 1) * step
                ]


def smooth_kernel(groups, places, nblk, *refs):
    inputs, pieces = len(places), groups * lax.axis_size("mem")
    in_refs, out_refs = refs[:inputs], refs[inputs : inputs + groups]
    keys_ref, tags_ref = refs[inputs + groups :]
    size = nblk * CAP + 8
    width = nblk * LANES
    for ref, blocks in zip(in_refs, places):
        for k, p in enumerate(blocks):
            if p is None:
                continue
            at = k * size
            for b in range(nblk):
                keys_ref[b, p * CAP : (p + 1) * CAP, :] = ref[at + b * CAP : at + (b + 1) * CAP, :]
            tags_ref[p : p + 1, :] = ref[at + nblk * CAP : at + nblk * CAP + 1, :].astype(jnp.float32)
    slots, count = groups * CAP, pieces * CAP
    keys = jnp.concatenate([keys_ref[b] for b in range(nblk)], axis=1)
    queries = keys[:slots]
    tags = spread(tags_ref[...], pieces)
    ktags = lax.dot_general(
        jnp.ones((8, LANES), jnp.bfloat16),
        tags.astype(jnp.bfloat16),
        (((1,), (1,)), ((), ())),
        preferred_element_type=jnp.float32,
    )[:1]
    qtags = jnp.sum(tags[:slots], axis=1, keepdims=True)
    sims = (
        lax.dot_general(
            queries, keys, (((1,), (1,)), ((), ())), preferred_element_type=jnp.float32
        )
    )
    keep = (
        (qtags == ktags)
        & (qtags >= 0.0)
        & (
            lax.broadcasted_iota(jnp.int32, (slots, count), 0)
            != lax.broadcasted_iota(jnp.int32, (slots, count), 1)
        )
    )
    weights = jnp.where(keep, jnp.exp(sims * (8.0 / width) - 8.0), 0.0)
    den = 1.0 + jnp.sum(weights, axis=1, keepdims=True)
    num = jnp.dot(weights.astype(jnp.bfloat16), keys, preferred_element_type=jnp.float32)
    result = ((queries.astype(jnp.float32) + num) * (1.0 / den)).astype(jnp.bfloat16)
    for s, mass_row in enumerate(gather_lanes(jnp.log(den), groups)):
        for b in range(nblk):
            out_refs[s][b * CAP : (b + 1) * CAP, :] = result[
                s * CAP : (s + 1) * CAP, b * LANES : (b + 1) * LANES
            ]
        out_refs[s][nblk * CAP :, :] = jnp.broadcast_to(mass_row, (8, LANES)).astype(jnp.bfloat16)


def unpack_kernel(steps, nblk, select_ref, *refs):
    groups = len(steps)
    in_refs, (smoothed_ref, mass_ref, back_ref, masses_ref) = refs[:groups], refs[groups:]
    for s, ref in zip(steps, in_refs):
        for b in range(nblk):
            back_ref[b, s * CAP : (s + 1) * CAP, :] = ref[b * CAP : (b + 1) * CAP, :]
        masses_ref[s : s + 1, :] = ref[nblk * CAP : nblk * CAP + 1, :].astype(jnp.float32)
    select = select_ref[...]
    over_slots = (((0,), (0,)), ((), ()))
    back = jnp.concatenate([back_ref[b] for b in range(nblk)], axis=1)
    smoothed_ref[...] = lax.dot_general(
        select, back, over_slots, preferred_element_type=jnp.float32
    ).astype(jnp.bfloat16)
    masses = spread(masses_ref[...], groups).astype(jnp.bfloat16)
    mass = lax.dot_general(masses, select, over_slots, preferred_element_type=jnp.float32)
    mass_ref[...] = jnp.sum(mass, axis=0).astype(jnp.bfloat16)


def gate(value, *after):
    if not after:
        return value
    return lax.optimization_barrier((value, *after))[0]


def off_chip(values):
    return [pltpu.with_memory_space_constraint(v, pltpu.HBM) for v in values]


def on_chip(values):
    return [pltpu.with_memory_space_constraint(v, pltpu.VMEM) for v in values]


def local(codes, scales, cluster_id):
    rows, width = codes.shape
    nblk = scales.shape[1]
    groups, members = lax.axis_size("grp"), lax.axis_size("mem")
    slots = groups * CAP
    size = nblk * CAP + 8
    piece = pltpu.VMEM((size, LANES), jnp.bfloat16)
    half, sides = groups // 2, members // 2
    near, far = list(range(1, half)), list(range(half, groups))

    def swap(value, axis, step):
        count = lax.axis_size(axis)
        return lax.ppermute(value, axis, [(i, i ^ step) for i in range(count)])

    def join(values):
        return jnp.concatenate(values) if len(values) > 1 else values[0]

    select, *outbox = pl.pallas_call(
        functools.partial(pack_kernel, groups),
        out_shape=[pltpu.VMEM((slots, rows), jnp.bfloat16)] + [piece] * groups,
        in_specs=[HBM] * 3,
        out_specs=[VMEM] * (1 + groups),
        scratch_shapes=[
            pltpu.VMEM(codes.shape, codes.dtype),
            pltpu.VMEM((nblk, rows), scales.dtype),
            pltpu.VMEM((1, rows), cluster_id.dtype),
            pltpu.SemaphoreType.DMA((3,)),
        ],
        compiler_params=ROOM,
        name="pack",
    )(*off_chip([codes, scales.T, cluster_id.reshape(1, rows)]))

    held = []

    def hold(value, where):
        held.append((value, where))
        return held[-1]

    def across(parts, *after):
        joined = gate(join([v for v, _ in parts]), *after)
        where = [w for _, ws in parts for w in ws]
        return [
            (swap(joined, "mem", step), [(s, step // 2) for s, _ in where]) for step in range(2, members, 2)
        ], joined

    def partner(parts, *after):
        joined = gate(join([v for v, _ in parts]), *after)
        return (swap(joined, "mem", 1), [(s, i + sides) for _, ws in parts for s, i in ws])

    def grp(s, *after):
        return (swap(gate(outbox[s], *after), "grp", s), [(s, 0)])

    got = {0: (outbox[0], [(0, 0)])}
    early, late = far[: half // 2], far[half // 2 :]
    for s in early[:1] + [1] + near[1:2] + early[1:]:
        got[s] = grp(s)
    ready = [got[0], got[1]]
    first, joined = across(ready)
    for s in near[2:] + late:
        got[s] = grp(s, joined)
    mid = [got[s] for s in near[1:] + early]
    second, _ = across(mid, joined)
    third, last = across([got[s] for s in late])
    held = [got[s] for s in early[:1] + [1] + near[1:2] + early[1:] + near[2:] + late] + first + second + third + [got[0]]
    held += [partner(ready + mid[:1]), partner(mid[1:] + first)]
    held += [partner([got[s] for s in late])]
    held += [partner([h]) for h in second + third]
    steps = [s for pair in zip(far, near + [0]) for s in pair]
    places = [[i * groups + steps.index(s) for s, i in where] for _, where in held]
    pieces = groups * members
    results = pl.pallas_call(
        functools.partial(smooth_kernel, groups, places, nblk),
        out_shape=[piece] * groups,
        in_specs=[VMEM] * len(held),
        out_specs=[VMEM] * groups,
        scratch_shapes=[
            pltpu.VMEM((nblk, pieces * CAP, LANES), jnp.bfloat16),
            pltpu.VMEM((pieces, LANES), jnp.float32),
        ],
        compiler_params=ROOM,
        name="smooth",
    )(*on_chip([v for v, _ in held]))
    result = dict(zip(steps, results))
    back = {s: swap(result[s], "grp", s) if s else result[s] for s in steps}
    done = steps
    smoothed, mass = pl.pallas_call(
        functools.partial(unpack_kernel, done, nblk),
        out_shape=[
            jax.ShapeDtypeStruct((rows, width), jnp.bfloat16),
            jax.ShapeDtypeStruct((rows,), jnp.bfloat16),
        ],
        in_specs=[VMEM] * (1 + groups),
        out_specs=[VMEM] * 2,
        scratch_shapes=[
            pltpu.VMEM((nblk, slots, LANES), jnp.bfloat16),
            pltpu.VMEM((groups, LANES), jnp.float32),
        ],
        compiler_params=ROOM,
        name="unpack",
    )(*on_chip([select] + [back[s] for s in done]))
    return (smoothed, mass)


def solution(mesh):
    placed = (P(("grp", "mem"), None), P(("grp", "mem"), None), P(("grp", "mem")))
    return jax.shard_map(
        local,
        mesh=mesh,
        in_specs=placed,
        out_specs=(P(("grp", "mem"), None), P(("grp", "mem"))),
        check_vma=False,
    )
```

```python
import functools

import jax
import jax.numpy as jnp
from jax import lax
from jax.experimental import pallas as pl
from jax.experimental.pallas import tpu as pltpu
from jax.sharding import PartitionSpec as P

CAP = 40
LANES = 128
VMEM = pl.BlockSpec(memory_space=pltpu.VMEM)
HBM = pl.BlockSpec(memory_space=pltpu.HBM)
ROOM = pltpu.CompilerParams(vmem_limit_bytes=24 * 2**20)


def as_column(row):
    n = row.shape[1]
    same = lax.broadcasted_iota(jnp.int32, (n, n), 0) == lax.broadcasted_iota(jnp.int32, (n, n), 1)
    return jnp.sum(jnp.where(same, jnp.broadcast_to(row, (n, n)), 0.0), axis=1, keepdims=True)


def slot_mask(slots):
    row = lax.broadcasted_iota(jnp.int32, (slots, LANES), 0)
    return lax.rem(row, CAP) == lax.broadcasted_iota(jnp.int32, (slots, LANES), 1)


def spread(rows_of_pieces, pieces):
    slots = pieces * CAP
    owner = lax.div(lax.broadcasted_iota(jnp.int32, (slots, pieces), 0), CAP)
    pick = jnp.where(owner == lax.broadcasted_iota(jnp.int32, (slots, pieces), 1), 1.0, 0.0)
    wide = jnp.dot(
        pick.astype(jnp.bfloat16), rows_of_pieces.astype(jnp.bfloat16), preferred_element_type=jnp.float32
    )
    return jnp.where(slot_mask(slots), wide, 0.0)


def gather_lanes(column, pieces):
    wide = jnp.where(slot_mask(pieces * CAP), column, 0.0)
    return [jnp.sum(wide[p * CAP : (p + 1) * CAP], axis=0, keepdims=True) for p in range(pieces)]


def pack_kernel(groups, codes_hbm, scales_hbm, cluster_hbm, select_ref, *refs):
    out_refs, (codes_ref, scales_ref, cluster_ref, sems) = refs[:groups], refs[groups:]
    copies = [
        pltpu.make_async_copy(src, dst, sems.at[i])
        for i, (src, dst) in enumerate(
            ((cluster_hbm, cluster_ref), (scales_hbm, scales_ref), (codes_hbm, codes_ref))
        )
    ]
    for copy in copies:
        copy.start()
    rows, width = codes_ref.shape
    nblk = scales_ref.shape[0]
    step = width // nblk
    copies[0].wait()
    cluster = cluster_ref[...]
    owner = lax.rem(cluster, groups)
    step_row = lax.bitwise_xor(owner, lax.axis_index("grp"))
    step_f = step_row.astype(jnp.float32)
    step_col = as_column(step_f)
    before = lax.broadcasted_iota(jnp.int32, (rows, rows), 0) < lax.broadcasted_iota(
        jnp.int32, (rows, rows), 1
    )
    rank = jnp.sum(
        jnp.where(before & (step_col == step_f), 1.0, 0.0), axis=0, keepdims=True
    ).astype(jnp.int32)
    target = step_row * CAP + rank
    slots = groups * CAP
    hit = lax.broadcasted_iota(jnp.int32, (slots, rows), 0) == target
    select = jnp.where(hit, 1.0, 0.0).astype(jnp.bfloat16)
    select_ref[...] = select
    tags = jnp.sum(jnp.where(hit, cluster.astype(jnp.float32) + 1.0, 0.0), axis=1, keepdims=True)
    for s, tag_row in enumerate(gather_lanes(tags, groups)):
        out_refs[s][nblk * CAP :, :] = jnp.broadcast_to(tag_row - 1.0, (8, LANES)).astype(jnp.bfloat16)
    copies[1].wait()
    copies[2].wait()
    scales = scales_ref[...].T
    parts = []
    total = None
    for b in range(nblk):
        x = codes_ref[:, b * step : (b + 1) * step].astype(jnp.float32) * scales[:, b : b + 1]
        parts.append(x)
        square = x * x
        total = square if total is None else total + square
    inv = lax.rsqrt(jnp.sum(total, axis=1, keepdims=True) / width + 1e-06)
    for at in range(0, nblk, 8):
        e = jnp.concatenate([(x * inv).astype(jnp.bfloat16) for x in parts[at : at + 8]], axis=1)
        packed = jnp.dot(select, e, preferred_element_type=jnp.float32).astype(jnp.bfloat16)
        for k in range(e.shape[1] // step):
            b = at + k
            for s in range(groups):
                out_refs[s][b * CAP : (b + 1) * CAP, :] = packed[
                    s * CAP : (s + 1) * CAP, k * step : (k + 1) * step
                ]


def smooth_kernel(groups, places, nblk, *refs):
    inputs, pieces = len(places), groups * lax.axis_size("mem")
    in_refs, out_refs = refs[:inputs], refs[inputs : inputs + groups]
    keys_ref, tags_ref = refs[inputs + groups :]
    size = nblk * CAP + 8
    width = nblk * LANES
    for ref, blocks in zip(in_refs, places):
        for k, p in enumerate(blocks):
            if p is None:
                continue
            at = k * size
            for b in range(nblk):
                keys_ref[b, p * CAP : (p + 1) * CAP, :] = ref[at + b * CAP : at + (b + 1) * CAP, :]
            tags_ref[p : p + 1, :] = ref[at + nblk * CAP : at + nblk * CAP + 1, :].astype(jnp.float32)
    slots, count = groups * CAP, pieces * CAP
    keys = jnp.concatenate([keys_ref[b] for b in range(nblk)], axis=1)
    queries = keys[:slots]
    tags = spread(tags_ref[...], pieces)
    ktags = lax.dot_general(
        jnp.ones((8, LANES), jnp.bfloat16),
        tags.astype(jnp.bfloat16),
        (((1,), (1,)), ((), ())),
        preferred_element_type=jnp.float32,
    )[:1]
    qtags = jnp.sum(tags[:slots], axis=1, keepdims=True)
    sims = (
        lax.dot_general(
            queries, keys, (((1,), (1,)), ((), ())), preferred_element_type=jnp.float32
        )
    )
    keep = (
        (qtags == ktags)
        & (qtags >= 0.0)
        & (
            lax.broadcasted_iota(jnp.int32, (slots, count), 0)
            != lax.broadcasted_iota(jnp.int32, (slots, count), 1)
        )
    )
    weights = jnp.where(keep, jnp.exp(sims * (8.0 / width) - 8.0), 0.0)
    den = 1.0 + jnp.sum(weights, axis=1, keepdims=True)
    num = jnp.dot(weights.astype(jnp.bfloat16), keys, preferred_element_type=jnp.float32)
    result = ((queries.astype(jnp.float32) + num) * (1.0 / den)).astype(jnp.bfloat16)
    for s, mass_row in enumerate(gather_lanes(jnp.log(den), groups)):
        for b in range(nblk):
            out_refs[s][b * CAP : (b + 1) * CAP, :] = result[
                s * CAP : (s + 1) * CAP, b * LANES : (b + 1) * LANES
            ]
        out_refs[s][nblk * CAP :, :] = jnp.broadcast_to(mass_row, (8, LANES)).astype(jnp.bfloat16)


def unpack_kernel(steps, nblk, select_ref, *refs):
    groups = len(steps)
    in_refs, (smoothed_ref, mass_ref, back_ref, masses_ref) = refs[:groups], refs[groups:]
    for s, ref in zip(steps, in_refs):
        for b in range(nblk):
            back_ref[b, s * CAP : (s + 1) * CAP, :] = ref[b * CAP : (b + 1) * CAP, :]
        masses_ref[s : s + 1, :] = ref[nblk * CAP : nblk * CAP + 1, :].astype(jnp.float32)
    select = select_ref[...]
    over_slots = (((0,), (0,)), ((), ()))
    back = jnp.concatenate([back_ref[b] for b in range(nblk)], axis=1)
    smoothed_ref[...] = lax.dot_general(
        select, back, over_slots, preferred_element_type=jnp.float32
    ).astype(jnp.bfloat16)
    masses = spread(masses_ref[...], groups).astype(jnp.bfloat16)
    mass = lax.dot_general(masses, select, over_slots, preferred_element_type=jnp.float32)
    mass_ref[...] = jnp.sum(mass, axis=0).astype(jnp.bfloat16)


def gate(value, *after):
    if not after:
        return value
    return lax.optimization_barrier((value, *after))[0]


def off_chip(values):
    return [pltpu.with_memory_space_constraint(v, pltpu.HBM) for v in values]


def on_chip(values):
    return [pltpu.with_memory_space_constraint(v, pltpu.VMEM) for v in values]


def local(codes, scales, cluster_id):
    rows, width = codes.shape
    nblk = scales.shape[1]
    groups, members = lax.axis_size("grp"), lax.axis_size("mem")
    slots = groups * CAP
    size = nblk * CAP + 8
    piece = pltpu.VMEM((size, LANES), jnp.bfloat16)
    half, sides = groups // 2, members // 2
    near, far = list(range(1, half)), list(range(half, groups))
    far = far[:-2] + far[:-3:-1]

    def swap(value, axis, step):
        count = lax.axis_size(axis)
        return lax.ppermute(value, axis, [(i, i ^ step) for i in range(count)])

    def join(values):
        return jnp.concatenate(values) if len(values) > 1 else values[0]

    select, *outbox = pl.pallas_call(
        functools.partial(pack_kernel, groups),
        out_shape=[pltpu.VMEM((slots, rows), jnp.bfloat16)] + [piece] * groups,
        in_specs=[HBM] * 3,
        out_specs=[VMEM] * (1 + groups),
        scratch_shapes=[
            pltpu.VMEM(codes.shape, codes.dtype),
            pltpu.VMEM((nblk, rows), scales.dtype),
            pltpu.VMEM((1, rows), cluster_id.dtype),
            pltpu.SemaphoreType.DMA((3,)),
        ],
        compiler_params=ROOM,
        name="pack",
    )(*off_chip([codes, scales.T, cluster_id.reshape(1, rows)]))

    held = []

    def hold(value, where):
        held.append((value, where))
        return held[-1]

    def across(parts, *after):
        joined = gate(join([v for v, _ in parts]), *after)
        where = [w for _, ws in parts for w in ws]
        return [
            (swap(joined, "mem", step), [(s, step // 2) for s, _ in where]) for step in range(2, members, 2)
        ], joined

    def partner(parts, *after):
        joined = gate(join([v for v, _ in parts]), *after)
        return (swap(joined, "mem", 1), [(s, i + sides) for _, ws in parts for s, i in ws])

    def grp(s, *after):
        return (swap(gate(outbox[s], *after), "grp", s), [(s, 0)])

    got = {0: (outbox[0], [(0, 0)])}
    early, late = far[: half // 2], far[half // 2 :]
    for s in early[:1] + [1] + near[1:2] + early[1:]:
        got[s] = grp(s)
    ready = [got[0], got[1]]
    first, joined = across(ready)
    for s in near[2:] + late:
        got[s] = grp(s, joined)
    mid = [got[s] for s in near[1:] + early]
    second, _ = across(mid, joined)
    third, last = across([got[s] for s in late])
    held = [got[s] for s in early[:1] + [1] + near[1:2] + early[1:] + near[2:] + late] + first + second + third + [got[0]]
    held += [partner(ready + mid[:1]), partner(mid[1:] + first)]
    held += [partner([got[s] for s in late])]
    held += [partner([h]) for h in second + third]
    steps = [s for pair in zip(far, near + [0]) for s in pair]
    places = [[i * groups + steps.index(s) for s, i in where] for _, where in held]
    pieces = groups * members
    results = pl.pallas_call(
        functools.partial(smooth_kernel, groups, places, nblk),
        out_shape=[piece] * groups,
        in_specs=[VMEM] * len(held),
        out_specs=[VMEM] * groups,
        scratch_shapes=[
            pltpu.VMEM((nblk, pieces * CAP, LANES), jnp.bfloat16),
            pltpu.VMEM((pieces, LANES), jnp.float32),
        ],
        compiler_params=ROOM,
        name="smooth",
    )(*on_chip([v for v, _ in held]))
    result = dict(zip(steps, results))
    back = {s: swap(result[s], "grp", s) if s else result[s] for s in steps}
    done = steps
    smoothed, mass = pl.pallas_call(
        functools.partial(unpack_kernel, done, nblk),
        out_shape=[
            jax.ShapeDtypeStruct((rows, width), jnp.bfloat16),
            jax.ShapeDtypeStruct((rows,), jnp.bfloat16),
        ],
        in_specs=[VMEM] * (1 + groups),
        out_specs=[VMEM] * 2,
        scratch_shapes=[
            pltpu.VMEM((nblk, slots, LANES), jnp.bfloat16),
            pltpu.VMEM((groups, LANES), jnp.float32),
        ],
        compiler_params=ROOM,
        name="unpack",
    )(*on_chip([select] + [back[s] for s in done]))
    return (smoothed, mass)


def solution(mesh):
    placed = (P(("grp", "mem"), None), P(("grp", "mem"), None), P(("grp", "mem")))
    return jax.shard_map(
        local,
        mesh=mesh,
        in_specs=placed,
        out_specs=(P(("grp", "mem"), None), P(("grp", "mem"))),
        check_vma=False,
    )
```
